1024 devices in a mesh: ctx: 128 (over z, x_hi, core), fsdp: 8 (over y, x_lo).
Axes of the slice: x: 4 (x_hi: 2, x_lo: 2; x = x_hi * 2 + x_lo), y: 4, z: 32, core: 2. Of those that a mesh axis runs over, the one named last changes fastest.
Arguments:
- queries: bfloat16 [65536, 2048], P('ctx', 'fsdp'), may hold values from -30 to 30
- keys: bfloat16 [65536, 2048], P('ctx', 'fsdp'), may hold values from -10 to 10
- values: bfloat16 [65536, 2048], P('ctx', 'fsdp'), may hold values from -16 to 16
- norm_gain: float32 [2048], P('fsdp'), may hold values from 0.25 to 1.75
- short_filters: float32 [3, 3, 2048], P(None, None, 'fsdp'), may hold values from -3 to 3
- medium_filters: bfloat16 [128, 128], P(None, 'fsdp'), may hold values from -0.5 to 0.5
Outputs:
- mixed: bfloat16 [65536, 2048], P('ctx', 'fsdp')
The draws below stay inside these ranges and needn't reach their ends.
All inputs are finite; a program needn't handle non-finite values.
Results may differ from the reference program's by a relative error of at most 0.012.
Values may be sent and summed in bfloat16 or wider, within the bound.
No kernel may reach another device: no remote copies, remote signals or barrier semaphores. Data moves between devices by JAX's collectives and lax.ppermute only.
A program may use at most 32 MiB of HBM per device.

```python
import math
import jax
import jax.numpy as jnp
from jax import lax

HEAD_DIM = 128
TOK_DEV = 512
TAPS = 128
SHORT = 3
GROUP_SIZE = 16
CHANNELS = 2048
SEQ = 65536
WINDOW = 1024


def draw_keys(key, part):
    base = jnp.clip(jax.random.normal(jax.random.fold_in(key, 11), (SEQ, CHANNELS), jnp.float32), -6.0, 6.0)
    return base.astype(jnp.bfloat16)


def draw_queries(key, part):
    base = jnp.clip(jax.random.normal(jax.random.fold_in(key, 13), (SEQ, CHANNELS), jnp.float32), -6.0, 6.0)
    return base.astype(jnp.bfloat16)


def draw_values(key, part):
    column = jnp.arange(CHANNELS, dtype=jnp.float32)[None, :]
    rising = 1.0 + 2.0 * column / (CHANNELS - 1)
    base = jnp.clip(jax.random.normal(jax.random.fold_in(key, 17), (SEQ, CHANNELS), jnp.float32), -5.0, 5.0)
    return (base * rising).astype(jnp.bfloat16)


def levels(key, dims, cuts, low, largest):
    def one(position, blocks):
        heights = jax.random.uniform(jax.random.fold_in(jax.random.fold_in(key, 6), position), (blocks,), jnp.float32, low / len(cuts), largest / len(cuts))
        return jnp.repeat(jnp.exp(heights), dims[position] // blocks).reshape((-1,) + (1,) * (len(dims) - position - 1))

    gain = one(*cuts[0])
    for cut in cuts[1:]:
        gain = gain * one(*cut)
    return gain


def gaussian(rng, dims, scale, reach, shards=(), kind=jnp.bfloat16):
    result = jax.random.normal(rng, dims, jnp.float32) * scale
    if len(shards) > 0:
        result = levels(rng, dims, shards, -0.22, 0.18) * result
    return jnp.clip(result, min=-reach, max=reach).astype(kind)


def setup_inputs(seed: int = 0) -> dict:
    streams_of = jax.random.split(jax.random.key(seed), 7)
    return {
        "queries": draw_queries(jax.random.fold_in(streams_of[6], 71), 0),
        "keys": draw_keys(jax.random.fold_in(streams_of[6], 71), 0),
        "values": draw_values(jax.random.fold_in(streams_of[6], 71), 0),
        "norm_gain": jnp.clip(1.0 + 0.15 * jax.random.normal(streams_of[3], (CHANNELS,), jnp.float32), 0.25, 1.75),
        "short_filters": gaussian(streams_of[4], (3, SHORT, CHANNELS), 0.6, 3.0, ((2, 8),), jnp.float32),
        "medium_filters": gaussian(streams_of[5], (TAPS, CHANNELS // GROUP_SIZE), TAPS ** -0.5, 0.5, ((1, 8),)),
    }


negative_big = -1e+30
norm_epsilon = 1e-06

def one_head(operands):
    query_head, key_head, value_head = operands
    head_size = query_head.shape[1]
    key_padded = jnp.concatenate([jnp.zeros((WINDOW, head_size), key_head.dtype), key_head], axis=0)
    value_padded = jnp.concatenate([jnp.zeros((WINDOW, head_size), value_head.dtype), value_head], axis=0)

    def one_block(block_index):
        start = (block_index * TOK_DEV).astype(jnp.int32)
        query_block = lax.dynamic_slice_in_dim(query_head, start, TOK_DEV, 0).astype(jnp.float32)
        key_block = lax.dynamic_slice_in_dim(key_padded, start, WINDOW + TOK_DEV, 0).astype(jnp.float32)
        value_block = lax.dynamic_slice_in_dim(value_padded, start, WINDOW + TOK_DEV, 0).astype(jnp.float32)
        query_pos = start + jnp.arange(TOK_DEV, dtype=jnp.int32)
        key_pos = start - WINDOW + jnp.arange(WINDOW + TOK_DEV, dtype=jnp.int32)
        allowed = (key_pos[None, :] <= query_pos[:, None]) & (key_pos[None, :] > query_pos[:, None] - WINDOW) & (key_pos[None, :] >= 0)
        scores = jnp.dot(query_block, key_block.T, precision=lax.Precision.HIGHEST) / math.sqrt(HEAD_DIM)
        masked = jnp.where(allowed, scores, negative_big)
        peak = lax.optimization_barrier(jnp.max(masked, axis=1, keepdims=True))
        exponent = jnp.where(allowed, jnp.exp(masked - peak), 0.0)
        denom = lax.optimization_barrier(jnp.sum(exponent, axis=1))
        probs = exponent.astype(jnp.bfloat16).astype(jnp.float32)
        summed = jnp.dot(probs, value_block, precision=lax.Precision.HIGHEST)
        return summed / denom[:, None]
    blocks = lax.map(one_block, jnp.arange(SEQ // TOK_DEV, dtype=jnp.int32))
    return blocks.reshape(SEQ, head_size)

def reference(queries, keys, values, norm_gain, short_filters, medium_filters):
    length, channels = queries.shape
    head_count = channels // HEAD_DIM
    query_heads = queries.reshape(length, head_count, HEAD_DIM).transpose(1, 0, 2)
    key_heads = keys.reshape(length, head_count, HEAD_DIM).transpose(1, 0, 2)
    value_heads = values.reshape(length, head_count, HEAD_DIM).transpose(1, 0, 2)
    outputs = lax.map(one_head, (query_heads, key_heads, value_heads))
    attended = outputs.transpose(1, 0, 2).reshape(length, channels).astype(jnp.bfloat16)
    attended_f = attended.astype(jnp.float32)
    mean_square = lax.optimization_barrier(jnp.mean(attended_f * attended_f, axis=1, keepdims=True))
    normed = (attended_f * lax.rsqrt(mean_square + norm_epsilon) * norm_gain[None, :]).astype(jnp.bfloat16)
    normed_f = normed.astype(jnp.float32)
    taps_short = short_filters.shape[1]
    padded = jnp.concatenate([jnp.zeros((taps_short - 1, channels), jnp.float32), normed_f], axis=0)

    def one_branch(index):
        total = jnp.zeros((length, channels), jnp.float32)
        for tap in range(taps_short):
            window = padded[taps_short - 1 - tap:taps_short - 1 - tap + length]
            total = total + short_filters[index, tap][None, :] * window
        return total
    product = (one_branch(1) * one_branch(2)).astype(jnp.bfloat16)
    product_f = product.astype(jnp.float32)
    filters_full = jnp.repeat(medium_filters.astype(jnp.float32), GROUP_SIZE, axis=1)
    taps_long = medium_filters.shape[0]
    padded_long = jnp.concatenate([jnp.zeros((taps_long - 1, channels), jnp.float32), product_f], axis=0)

    def add_tap(tap, total):
        window = lax.dynamic_slice_in_dim(padded_long, (taps_long - 1 - tap).astype(jnp.int32), length, 0)
        return total + filters_full[tap][None, :] * window
    long_mix = lax.fori_loop(0, taps_long, add_tap, jnp.zeros((length, channels), jnp.float32))
    return (attended_f + one_branch(0) * long_mix).astype(jnp.bfloat16)
```

```python
import functools
import math

import jax
import jax.numpy as jnp
from jax import lax
from jax.experimental import pallas as pl
from jax.experimental.pallas import tpu as pltpu
from jax.sharding import PartitionSpec as P

HEAD_DIM = 128
BLOCK = 256
HALO = 144
NEG = -1e30
EPS = 1e-6
LOG2E = 1.4426950408889634
VMEM = pl.BlockSpec(memory_space=pltpu.VMEM)
HIGHEST = lax.Precision.HIGHEST


def attend_kernel(q_ref, k2_ref, v2_ref, k1_ref, v1_ref, k0_ref, v0_ref, out_ref, sq_ref):
    rows = q_ref.shape[0]
    heads = q_ref.shape[1] // HEAD_DIM
    blocks = rows // BLOCK
    scale = LOG2E / math.sqrt(HEAD_DIM)
    ctx = lax.axis_index("ctx")
    gone1 = jnp.where(ctx >= 1, 0.0, -NEG).astype(jnp.float32)
    gone2 = jnp.where(ctx >= 2, 0.0, -NEG).astype(jnp.float32)
    ri = lax.broadcasted_iota(jnp.int32, (BLOCK, BLOCK), 0)
    ci = lax.broadcasted_iota(jnp.int32, (BLOCK, BLOCK), 1)
    ones = jnp.ones((8, HEAD_DIM), jnp.float32)
    for qb in range(blocks):
        squares = None
        for h in range(heads):
            cols = slice(h * HEAD_DIM, (h + 1) * HEAD_DIM)
            q = q_ref[qb * BLOCK : (qb + 1) * BLOCK, cols]
            groups = (
                (k2_ref, v2_ref, range(qb, blocks), ci > ri, gone2),
                (k1_ref, v1_ref, range(blocks), None, gone1),
                (k0_ref, v0_ref, range(qb + 1), ci <= ri, None),
            )
            peak = None
            scores = []
            for k_ref, v_ref, which, mask, gone in groups:
                top = None
                for j in which:
                    at = slice(j * BLOCK, (j + 1) * BLOCK)
                    s = lax.dot_general(
                        q, k_ref[at, cols], (((1,), (1,)), ((), ())),
                        preferred_element_type=jnp.float32,
                    )
                    if mask is not None and j == qb:
                        s = jnp.where(mask, s, NEG)
                    scores.append((s, v_ref, at, gone))
                    for w in range(0, BLOCK, 128):
                        part = s[:, w : w + 128]
                        top = part if top is None else jnp.maximum(top, part)
                if gone is not None:
                    top = top - gone
                peak = top if peak is None else jnp.maximum(peak, top)
            peak = jnp.max(peak, axis=1, keepdims=True)
            total = None
            acc = None
            for s, v_ref, at, gone in scores:
                off = peak if gone is None else peak + gone
                p = jnp.exp2((s - off) * scale)
                for w in range(0, BLOCK, 128):
                    part = p[:, w : w + 128]
                    total = part if total is None else total + part
                o = jnp.dot(
                    p.astype(jnp.bfloat16), v_ref[at, cols], preferred_element_type=jnp.float32
                )
                acc = o if acc is None else acc + o
            denom = jnp.sum(total, axis=1, keepdims=True)
            att = (acc / denom).astype(jnp.bfloat16)
            out_ref[qb * BLOCK : (qb + 1) * BLOCK, cols] = att
            af = att.astype(jnp.float32)
            sq = lax.dot_general(
                ones, af * af, (((1,), (1,)), ((), ())),
                precision=HIGHEST, preferred_element_type=jnp.float32,
            )
            squares = sq if squares is None else squares + sq
        sq_ref[:, qb * BLOCK : (qb + 1) * BLOCK] = squares


def toeplitz_kernel(filt_ref, out_ref):
    taps, groups = filt_ref.shape
    tap = lax.broadcasted_iota(jnp.int32, (taps, 2 * taps), 0)
    ext = lax.broadcasted_iota(jnp.int32, (taps, 2 * taps), 1)
    flip = jnp.where(ext == taps - tap, 1.0, 0.0).astype(jnp.bfloat16)
    base = lax.dot_general(
        filt_ref[...], flip, (((0,), (0,)), ((), ())), preferred_element_type=jnp.float32
    )
    for g in range(groups):
        row = jnp.broadcast_to(base[g : g + 1, :], (taps, 2 * taps))
        table = pltpu.roll(row, 0, 1, stride=1, stride_axis=0)
        out_ref[g * taps : (g + 1) * taps, :] = table.astype(jnp.bfloat16)


def norm_kernel(total_channels, sq_ref, att_ref, gain_ref, out_ref, tail_ref):
    rows, channels = att_ref.shape
    ones = jnp.ones((sq_ref.shape[0], 128), jnp.float32)
    summed = lax.dot_general(
        sq_ref[...], ones, (((0,), (0,)), ((), ())),
        precision=HIGHEST, preferred_element_type=jnp.float32,
    )
    inverse = lax.rsqrt(summed / total_channels + EPS)
    for w in range(0, channels, 128):
        normed = (
            att_ref[:, w : w + 128].astype(jnp.float32) * inverse * gain_ref[:, w : w + 128]
        ).astype(jnp.bfloat16)
        out_ref[:, w : w + 128] = normed
        tail_ref[:, w : w + 128] = normed[rows - HALO :]


def mix_kernel(att_ref, normed_ref, halo_ref, short_ref, table_ref, out_ref, ext_ref, prod_ref):
    rows, channels = att_ref.shape
    taps = table_ref.shape[1] // 2
    per_lane_tile = 128 * table_ref.shape[0] // (taps * channels)
    ext_ref[:HALO, :] = halo_ref[...].astype(jnp.float32)
    ext_ref[HALO:, :] = normed_ref[...].astype(jnp.float32)
    first = HALO - taps

    def branch(b, start, size):
        total = short_ref[3 * b : 3 * b + 1, :] * ext_ref[start : start + size, :]
        for t in range(1, 3):
            total = total + short_ref[3 * b + t : 3 * b + t + 1, :] * ext_ref[start - t : start - t + size, :]
        return total

    for r in range(0, rows + taps, taps):
        prod_ref[r : r + taps, :] = (
            branch(1, first + r, taps) * branch(2, first + r, taps)
        ).astype(jnp.bfloat16)
    group = lax.broadcasted_iota(jnp.int32, (taps, 128), 1) // (128 // per_lane_tile)
    for r in range(0, rows, taps):
        query = branch(0, HALO + r, taps)
        for w in range(0, channels, 128):
            n = taps * per_lane_tile
            at = (w // 128) * n
            mixed = jnp.dot(
                table_ref[at : at + n, :], prod_ref[r : r + 2 * taps, w : w + 128],
                preferred_element_type=jnp.float32,
            )
            long_mix = mixed[:taps]
            for g in range(1, per_lane_tile):
                long_mix = jnp.where(group == g, mixed[g * taps : (g + 1) * taps], long_mix)
            out_ref[r : r + taps, w : w + 128] = (
                att_ref[r : r + taps, w : w + 128].astype(jnp.float32)
                + query[:, w : w + 128] * long_mix
            ).astype(jnp.bfloat16)


def shape(*dims, dtype=jnp.bfloat16):
    return jax.ShapeDtypeStruct(dims, dtype)


def call(kernel, out_shape, args, scratch=(), name=None, flops=0, nbytes=0, trans=0):
    outs = out_shape if isinstance(out_shape, tuple) else (out_shape,)
    result = pl.pallas_call(
        kernel,
        out_shape=outs,
        in_specs=[VMEM] * len(args),
        out_specs=tuple(VMEM for _ in outs),
        scratch_shapes=list(scratch),
        name=name,
        cost_estimate=pl.CostEstimate(flops=flops, bytes_accessed=nbytes, transcendentals=trans),
    )(*args)
    return result if isinstance(out_shape, tuple) else result[0]


def per_device(queries, keys, values, norm_gain, short_filters, medium_filters):
    rows, channels = queries.shape
    taps, groups = medium_filters.shape
    count = lax.axis_size("ctx")
    peers = lax.axis_size("fsdp")
    ctx = lax.axis_index("ctx")
    ahead = [(i, i + 2) for i in range(count - 2)]
    beside = [(i, i ^ 1) for i in range(count)]
    even = ctx % 2 == 0

    k2 = lax.ppermute(keys, "ctx", ahead)
    v2 = lax.ppermute(values, "ctx", ahead)
    k1 = lax.ppermute(jnp.where(even, keys, k2), "ctx", beside)
    v1 = lax.ppermute(jnp.where(even, values, v2), "ctx", beside)

    table = call(
        toeplitz_kernel, shape(groups * taps, 2 * taps), (medium_filters,), name="table",
        flops=1 << 20, nbytes=1 << 20,
    )
    attended, squares = call(
        attend_kernel,
        (shape(rows, channels), shape(peers, rows, dtype=jnp.float32)),
        (queries, k2, v2, k1, v1, keys, values),
        name="attend", flops=600 << 20, nbytes=2 << 20, trans=1 << 20,
    )
    shared = lax.all_to_all(squares, "fsdp", 0, 0, tiled=True)
    normed, tail = call(
        functools.partial(norm_kernel, channels * peers),
        (shape(rows, channels), shape(HALO, channels)),
        (shared, attended, norm_gain.reshape(1, channels)),
        name="norm", flops=1 << 20, nbytes=1 << 19,
    )
    halo = lax.ppermute(tail, "ctx", [(i, i + 1) for i in range(count - 1)])
    return call(
        mix_kernel, shape(rows, channels),
        (attended, normed, halo, short_filters.reshape(9, channels), table),
        scratch=(
            pltpu.VMEM((rows + HALO, channels), jnp.float32),
            pltpu.VMEM((rows + taps, channels), jnp.bfloat16),
        ),
        name="mix", flops=1 << 30, nbytes=2 << 20,
    )


def solution(mesh):
    placed = (
        P("ctx", "fsdp"),
        P("ctx", "fsdp"),
        P("ctx", "fsdp"),
        P("fsdp"),
        P(None, None, "fsdp"),
        P(None, "fsdp"),
    )
    return jax.shard_map(
        per_device, mesh=mesh, in_specs=placed, out_specs=P("ctx", "fsdp"), check_vma=False
    )
```

```python
import functools
import math

import jax
import jax.numpy as jnp
from jax import lax
from jax.experimental import pallas as pl
from jax.experimental.pallas import tpu as pltpu
from jax.sharding import PartitionSpec as P


HEAD_DIM = 128
BLOCK = 256
HALO = 144
NEG = -1e30
EPS = 1e-6
LOG2E = 1.4426950408889634
SCALE = LOG2E / math.sqrt(HEAD_DIM)
VMEM = pl.BlockSpec(memory_space=pltpu.VMEM)
HBM = pl.BlockSpec(memory_space=pltpu.HBM)
HIGHEST = lax.Precision.HIGHEST
F32 = jnp.float32
BF16 = jnp.bfloat16


def cols_of(h):
    return slice(h * HEAD_DIM, (h + 1) * HEAD_DIM)


def peak_of(unit):
    q, groups, state = unit
    rows = q.shape[0]
    scores = []
    peak = None
    for pieces, gone in groups:
        top = None
        for k, v, mask in pieces:
            s = lax.dot_general(q, k, (((1,), (1,)), ((), ())), preferred_element_type=F32)
            if mask is not None:
                s = jnp.where(mask, s, NEG)
            scores.append((s, v, gone))
            for w in range(0, BLOCK, 128):
                piece = s[:, w : w + 128]
                top = piece if top is None else jnp.maximum(top, piece)
        if gone is not None:
            top = top - gone
        peak = top if peak is None else jnp.maximum(peak, top)
    peak = jnp.broadcast_to(jnp.max(peak, axis=1, keepdims=True), (rows, 128))
    if state is not None:
        peak = jnp.maximum(state[0], peak)
    return scores, peak


def weigh(unit, scores, peak):
    total = acc = None
    if unit[2] is not None:
        before, total, acc = unit[2]
        shrink = jnp.exp2((before - peak) * SCALE)
        total, acc = total * shrink, acc * shrink
    for s, v, gone in scores:
        off = peak if gone is None else peak + gone
        halves = []
        for w in range(0, BLOCK, 128):
            p = jnp.exp2((s[:, w : w + 128] - off) * SCALE)
            total = p if total is None else total + p
            halves.append(p.astype(BF16))
        o = jnp.dot(jnp.concatenate(halves, axis=1), v, preferred_element_type=F32)
        acc = o if acc is None else acc + o
    return peak, total, acc


def run_units(units, done):
    ahead = peak_of(units[0][0])
    for i, (unit, tag) in enumerate(units):
        now = ahead
        if i + 1 < len(units):
            ahead = peak_of(units[i + 1][0])
        done(tag, weigh(unit, *now))


def finish(state):
    _, total, acc = state
    return (acc / jnp.sum(total, axis=1, keepdims=True)).astype(BF16)


def part(i):
    return slice(i * BLOCK, (i + 1) * BLOCK)


def grid_iota():
    shape = (BLOCK, BLOCK)
    return lax.broadcasted_iota(jnp.int32, shape, 0), lax.broadcasted_iota(jnp.int32, shape, 1)


def absent(distance):
    return jnp.where(lax.axis_index("ctx") >= distance, 0.0, -NEG).astype(F32)


def is_even():
    return lax.rem(lax.axis_index("ctx"), 2) == 0


def early_kernel(
    q_ref, k_ref, v_ref, filt_ref, short_ref, gain_ref, peak_ref, total_ref, acc_ref, table_ref,
    coef_ref,
):
    rows, channels = q_ref.shape
    ri, ci = grid_iota()
    units = []
    for h in range(channels // HEAD_DIM):
        cols = cols_of(h)
        for b in range(rows // BLOCK):
            pieces = [
                (k_ref[part(j), cols], v_ref[part(j), cols], ci <= ri if j == b else None)
                for j in range(b + 1)
            ]
            units.append(((q_ref[part(b), cols], [(pieces, None)], None), (part(b), cols)))

    def done(tag, state):
        peak_ref[tag], total_ref[tag], acc_ref[tag] = state

    run_units(units, done)
    groups, taps = filt_ref.shape
    tap = lax.broadcasted_iota(jnp.int32, (taps, 2 * taps), 0)
    ext = lax.broadcasted_iota(jnp.int32, (taps, 2 * taps), 1)
    flip = jnp.where(ext == taps - tap, 1.0, 0.0).astype(BF16)
    base = jnp.dot(filt_ref[...], flip, preferred_element_type=F32)
    for g in range(groups):
        row = jnp.broadcast_to(base[g : g + 1, :], (taps, 2 * taps))
        shifted = pltpu.roll(row, 0, 1, stride=1, stride_axis=0)
        table_ref[g * taps : (g + 1) * taps, :] = shifted.astype(BF16)
    for i in range(9):
        coef_ref[i : i + 1, :] = short_ref[i // 3, i % 3 : i % 3 + 1, :]
    coef_ref[9:10, :] = gain_ref[...]


def pick_keys_kernel(own_ref, far_ref, out_ref):
    rows = own_ref.shape[0]

    @pl.when(is_even())
    def _():
        out_ref[:rows, :] = own_ref[...]
        out_ref[rows:, :] = far_ref[rows - BLOCK :, :]

    @pl.when(jnp.logical_not(is_even()))
    def _():
        out_ref[:rows, :] = far_ref[...]


def pick_values_kernel(own_ref, far_ref, after_ref, out_ref):
    size = own_ref.shape[0]
    rows = size - HALO

    @pl.when(is_even())
    def _():
        out_ref[:size, :] = own_ref[...]
        out_ref[size:, :] = far_ref[rows - BLOCK : rows, :]

    @pl.when(jnp.logical_not(is_even()))
    def _():
        out_ref[:size, :] = far_ref[...]


def far_kernel(q_ref, k_ref, v_ref, peak_in, total_in, acc_in, peak_ref, total_ref, acc_ref):
    rows, channels = q_ref.shape
    blocks = rows // BLOCK
    gone = absent(2)
    ri, ci = grid_iota()
    units = []
    for h in range(channels // HEAD_DIM):
        cols = cols_of(h)
        for b in range(blocks):
            tag = (part(b), cols)
            pieces = [
                (k_ref[part(j), cols], v_ref[part(j), cols], ci > ri if j == b else None)
                for j in range(b, blocks)
            ]
            state = (peak_in[tag], total_in[tag], acc_in[tag])
            units.append(((q_ref[tag], [(pieces, gone)], state), tag))

    def done(tag, state):
        peak_ref[tag], total_ref[tag], acc_ref[tag] = state

    run_units(units, done)


def row_squares(att):
    af = att.astype(F32)
    af = af * af
    high = af.astype(BF16)
    low = (af - high.astype(F32)).astype(BF16)
    ones = jnp.ones((8, af.shape[1]), BF16)
    dims = (((1,), (1,)), ((), ()))
    return lax.dot_general(ones, high, dims, preferred_element_type=F32) + lax.dot_general(
        ones, low, dims, preferred_element_type=F32
    )


def near_kernel(
    q_ref, k2_ref, v2_ref, k1_ref, v1_ref, tails_ref, peak_in, total_in, acc_in,
    out_ref, halo_ref, sq_ref,
):
    rows, channels = q_ref.shape
    heads = channels // HEAD_DIM
    blocks = rows // BLOCK
    shift = BLOCK - HALO
    ri = lax.broadcasted_iota(jnp.int32, (HALO, BLOCK), 0)
    ci = lax.broadcasted_iota(jnp.int32, (HALO, BLOCK), 1)
    sq_ref[:, 0, :BLOCK] = jnp.zeros((sq_ref.shape[0], BLOCK), F32)
    units = []
    for h in range(heads):
        cols = cols_of(h)
        k3 = jnp.where(is_even(), tails_ref[:BLOCK, cols], k1_ref[rows:, cols])
        v3 = jnp.where(is_even(), tails_ref[BLOCK:, cols], v1_ref[rows + HALO :, cols])
        near = [(k1_ref[part(j), cols], v1_ref[part(j), cols], None) for j in range(blocks)]
        near[-1] = (*near[-1][:2], ci <= ri + shift)
        middle = [(k2_ref[part(j), cols], v2_ref[part(j), cols], None) for j in range(blocks)]
        groups = [
            (near, absent(1)),
            (middle, absent(2)),
            ([(k3, v3, ci > ri + shift)], absent(3)),
        ]
        units.append(((v1_ref[rows : rows + HALO, cols], groups, None), (None, h)))
    for b in range(blocks):
        for h in range(heads):
            cols = cols_of(h)
            tag = (part(b), cols)
            near = [(k1_ref[part(j), cols], v1_ref[part(j), cols], None) for j in range(blocks)]
            state = (peak_in[tag], total_in[tag], acc_in[tag])
            units.append(((q_ref[tag], [(near, absent(1))], state), (b, h)))

    def done(tag, state):
        b, h = tag
        att = finish(state)
        if b is None:
            halo_ref[:, cols_of(h)] = jnp.where(
                lax.axis_index("ctx") >= 1, att, jnp.zeros(att.shape, BF16)
            )
            if h == heads - 1:
                sq_ref[:, 0, :HALO] = row_squares(halo_ref[...])
        else:
            out_ref[part(b), cols_of(h)] = att
            if h == heads - 1:
                sq_ref[:, 0, part(b + 1)] = row_squares(out_ref[part(b), :])

    run_units(units, done)


def mix_kernel(total_channels, sq_ref, halo_ref, att_ref, coef_ref, table_ref, out_ref, ext_ref, prod_ref):
    rows, channels = att_ref.shape
    taps = table_ref.shape[1] // 2
    per_lane_tile = 128 * table_ref.shape[0] // (taps * channels)
    ones = jnp.ones((sq_ref.shape[0], 128), F32)
    summed = lax.dot_general(
        sq_ref[:, 0, :], ones, (((0,), (0,)), ((), ())),
        precision=HIGHEST, preferred_element_type=F32,
    )
    inverse = lax.rsqrt(summed / total_channels + EPS)
    for ref, at, size, start in ((halo_ref, 0, HALO, 0), (att_ref, HALO, rows, BLOCK)):
        for w in range(0, channels, 128):
            lanes = slice(w, w + 128)
            normed = (
                ref[:, lanes].astype(F32) * inverse[start : start + size] * coef_ref[9:10, lanes]
            ).astype(BF16)
            ext_ref[at : at + size, lanes] = normed.astype(F32)

    def branch(b, start, size, lanes=slice(None)):
        total = coef_ref[3 * b : 3 * b + 1, lanes] * ext_ref[start : start + size, lanes]
        for t in range(1, 3):
            total = total + coef_ref[3 * b + t : 3 * b + t + 1, lanes] * ext_ref[start - t : start - t + size, lanes]
        return total

    for r in range(0, rows + taps, taps):
        start = HALO - taps + r
        prod_ref[r : r + taps, :] = (branch(1, start, taps) * branch(2, start, taps)).astype(BF16)
    group = lax.broadcasted_iota(jnp.int32, (taps, 128), 1) // (128 // per_lane_tile)
    n = taps * per_lane_tile
    for w in range(0, channels, 128):
        lanes = slice(w, w + 128)
        at = (w // 128) * n
        for r in range(0, rows, 2 * taps):
            pair = jnp.concatenate(
                [prod_ref[r + d : r + d + 2 * taps, lanes] for d in (0, taps)], axis=1
            )
            mixed = jnp.dot(table_ref[at : at + n, :], pair, preferred_element_type=F32)
            for i in range(2):
                ri = r + i * taps
                long_mix = mixed[:taps, i * 128 : (i + 1) * 128]
                for g in range(1, per_lane_tile):
                    long_mix = jnp.where(
                        group == g, mixed[g * taps : (g + 1) * taps, i * 128 : (i + 1) * 128], long_mix
                    )
                query = branch(0, HALO + ri, taps, lanes)
                out_ref[ri : ri + taps, lanes] = (
                    att_ref[ri : ri + taps, lanes].astype(F32) + query * long_mix
                ).astype(BF16)


def array(*dims, dtype=BF16):
    return jax.ShapeDtypeStruct(dims, dtype)


def call(kernel, out_shape, args, scratch=(), flops=0, mib=8, spec=VMEM):
    outs = out_shape if isinstance(out_shape, tuple) else (out_shape,)
    nbytes = sum(math.prod(a.shape) * a.dtype.itemsize for a in (*args, *outs))
    result = pl.pallas_call(
        kernel,
        out_shape=outs,
        in_specs=[spec] * len(args),
        out_specs=tuple(VMEM for _ in outs),
        scratch_shapes=list(scratch),
        cost_estimate=pl.CostEstimate(flops=flops, bytes_accessed=nbytes, transcendentals=0),
        compiler_params=pltpu.CompilerParams(vmem_limit_bytes=mib << 20),
    )(*args)
    return result if isinstance(out_shape, tuple) else result[0]


def per_device(queries, keys, values, norm_gain, short_filters, medium_filters):
    rows, channels = queries.shape
    taps, groups = medium_filters.shape
    count = lax.axis_size("ctx")
    peers = lax.axis_size("fsdp")
    ahead = [(i, i + 2) for i in range(count - 2)]
    beside = [(i, i ^ 1) for i in range(count)]

    behind_three = [(i, i + 3) for i in range(1, count - 3, 2)]

    half = array(rows, channels)
    full = array(rows, channels, dtype=F32)
    k2 = lax.ppermute(keys, "ctx", ahead)
    vq = jnp.concatenate([values, queries[rows - HALO :]], axis=0)
    vq2 = lax.ppermute(vq, "ctx", ahead)
    tails = jnp.concatenate([keys[rows - BLOCK :], values[rows - BLOCK :]], axis=0)
    tails3 = lax.ppermute(tails, "ctx", behind_three)
    q, k = queries, keys
    picked = call(pick_keys_kernel, array(rows + BLOCK, channels), (k, k2))
    k1 = lax.ppermute(picked, "ctx", beside)
    peak, total, acc, table, coef = call(
        early_kernel,
        (full, full, full, array(groups * taps, 2 * taps), array(16, channels, dtype=F32)),
        (q, k, vq, medium_filters.T, short_filters, norm_gain.reshape(1, channels)),
        flops=300 << 20, mib=12,
    )
    picked = call(pick_values_kernel, array(rows + HALO + BLOCK, channels), (vq, vq2, peak))
    v1 = lax.ppermute(picked, "ctx", beside)
    peak, total, acc = call(
        far_kernel, (full, full, full), (q, k2, vq2, peak, total, acc),
        flops=300 << 20, mib=12,
    )
    attended, halo, squares = call(
        near_kernel, (half, array(HALO, channels), array(peers, 1, BLOCK + rows, dtype=F32)),
        (q, k2, vq2, k1, v1, tails3, peak, total, acc), flops=500 << 20, mib=16,
    )
    shared = lax.all_to_all(squares, "fsdp", 0, 0, tiled=True)
    return call(
        functools.partial(mix_kernel, channels * peers), half,
        (shared, halo, attended, coef, table),
        scratch=(
            pltpu.VMEM((rows + HALO, channels), F32),
            pltpu.VMEM((rows + taps, channels), BF16),
        ),
        flops=1 << 30, mib=12,
    )


def solution(mesh):
    placed = (
        P("ctx", "fsdp"),
        P("ctx", "fsdp"),
        P("ctx", "fsdp"),
        P("fsdp"),
        P(None, None, "fsdp"),
        P(None, "fsdp"),
    )

    return jax.shard_map(
        per_device, mesh=mesh, in_specs=placed, out_specs=P("ctx", "fsdp"), check_vma=False
    )
```

```python
import functools
import math

import jax
import jax.numpy as jnp
from jax import lax
from jax.experimental import pallas as pl
from jax.experimental.pallas import tpu as pltpu
from jax.sharding import PartitionSpec as P


HEAD_DIM = 128
BLOCK = 256
HALO = 144
TAIL = 128
NEG = -1e30
EPS = 1e-6
LOG2E = 1.4426950408889634
SCALE = LOG2E / math.sqrt(HEAD_DIM)
VMEM = pl.BlockSpec(memory_space=pltpu.VMEM)
HBM = pl.BlockSpec(memory_space=pltpu.HBM)
F32 = jnp.float32
BF16 = jnp.bfloat16


def cols_of(h):
    return slice(h * HEAD_DIM, (h + 1) * HEAD_DIM)


def peak_of(unit):
    q, groups, state = unit
    rows = q.shape[0]
    scores = []
    peak = None
    for pieces, gone in groups:
        top = None
        for k, v, mask in pieces:
            s = lax.dot_general(q, k, (((1,), (1,)), ((), ())), preferred_element_type=F32)
            if mask is not None:
                s = jnp.where(mask, s, NEG)
            scores.append((s, v, gone))
            for w in range(0, s.shape[1], 128):
                piece = s[:, w : w + 128]
                top = piece if top is None else jnp.maximum(top, piece)
        if gone is not None:
            top = top - gone
        peak = top if peak is None else jnp.maximum(peak, top)
    peak = jnp.broadcast_to(jnp.max(peak, axis=1, keepdims=True), (rows, 128))
    if state is not None:
        peak = jnp.maximum(state[0], peak)
    return scores, peak


def weigh(unit, scores, peak):
    total = acc = None
    if unit[2] is not None:
        before, total, acc = unit[2]
        shrink = jnp.exp2((before - peak) * SCALE)
        total, acc = total * shrink, acc * shrink
    for s, v, gone in scores:
        off = peak if gone is None else peak + gone
        halves = []
        for w in range(0, s.shape[1], 128):
            p = jnp.exp2((s[:, w : w + 128] - off) * SCALE)
            total = p if total is None else total + p
            halves.append(p.astype(BF16))
        o = jnp.dot(jnp.concatenate(halves, axis=1) if len(halves) > 1 else halves[0], v, preferred_element_type=F32)
        acc = o if acc is None else acc + o
    return peak, total, acc


def exponents(unit, scores, peak):
    shrink = total = None
    if unit[2] is not None:
        shrink = jnp.exp2((unit[2][0] - peak) * SCALE)
        total = unit[2][1] * shrink
    pieces = []
    for s, _, gone in scores:
        off = peak if gone is None else peak + gone
        for w in range(0, s.shape[1], 128):
            p = jnp.exp2((s[:, w : w + 128] - off) * SCALE)
            total = p if total is None else total + p
            pieces.append(p.astype(BF16))
    inverse = 1.0 / jnp.sum(total, axis=1, keepdims=True)
    return shrink, jnp.broadcast_to(inverse, total.shape), pieces


def run_units(units, then, done):
    ahead = peak_of(units[0][0])
    for i, (unit, tag) in enumerate(units):
        now = ahead
        if i + 1 < len(units):
            ahead = peak_of(units[i + 1][0])
        done(tag, then(unit, *now))


def finish(state):
    _, total, acc = state
    return (acc / jnp.sum(total, axis=1, keepdims=True)).astype(BF16)


def part(i):
    return slice(i * BLOCK, (i + 1) * BLOCK)


def grid_iota():
    shape = (BLOCK, BLOCK)
    return lax.broadcasted_iota(jnp.int32, shape, 0), lax.broadcasted_iota(jnp.int32, shape, 1)


def absent(distance):
    return jnp.where(lax.axis_index("ctx") >= distance, 0.0, -NEG).astype(F32)


def is_even():
    return lax.rem(lax.axis_index("ctx"), 2) == 0


def early_kernel(
    q_ref, k_ref, v_ref, peak_ref, total_ref, acc_ref,
):
    rows, channels = q_ref.shape
    ri, ci = grid_iota()
    units = []
    for h in range(channels // HEAD_DIM):
        cols = cols_of(h)
        for b in range(rows // BLOCK):
            pieces = [
                (k_ref[part(j), cols], v_ref[part(j), cols], ci <= ri if j == b else None)
                for j in range(b + 1)
            ]
            units.append(((q_ref[part(b), cols], [(pieces, None)], None), (part(b), cols)))

    def done(tag, state):
        peak_ref[tag], total_ref[tag], acc_ref[tag] = state

    run_units(units, weigh, done)


def pick_kernel(rows, own_ref, far_ref, *refs):
    out_ref = refs[-1]
    size = own_ref.shape[0]

    @pl.when(is_even())
    def _():
        out_ref[:size, :] = own_ref[...]
        out_ref[size:, :] = far_ref[rows - TAIL : rows, :]

    @pl.when(jnp.logical_not(is_even()))
    def _():
        out_ref[:size, :] = far_ref[...]


def score_kernel(
    q_ref, k2_ref, k1_ref, peak_in, total_in, near_ref, far_ref, shrink_ref, inv_ref
):
    rows, channels = q_ref.shape
    heads = channels // HEAD_DIM
    blocks = rows // BLOCK
    ri, ci = grid_iota()
    units = []
    for b in range(blocks):
        for h in range(heads):
            cols = cols_of(h)
            tag = (part(b), cols)
            near = [(k1_ref[part(j), cols], None, None) for j in range(blocks)]
            far = [
                (k2_ref[part(j), cols], None, ci > ri if j == b else None)
                for j in range(b, blocks)
            ]
            state = (peak_in[tag], total_in[tag], None)
            units.append(((q_ref[tag], [(near, absent(1)), (far, absent(2))], state), (b, h)))

    def done(tag, result):
        b, h = tag
        shrink, inverse, pieces = result
        shrink_ref[part(b), cols_of(h)] = shrink
        inv_ref[part(b), cols_of(h)] = inverse
        for i, p in enumerate(pieces):
            key = i * 128
            ref = near_ref
            if key >= rows:
                ref, key = far_ref, key - rows + b * BLOCK
            ref[part(b), h * rows + key : h * rows + key + 128] = p

    run_units(units, exponents, done)


def far_values_kernel(
    far_ref, shrink_ref, acc_ref, v2_ref, filt_ref, short_ref, gain_ref, out_ref, table_ref, coef_ref
):
    rows, channels = acc_ref.shape
    for h in range(channels // HEAD_DIM):
        cols = cols_of(h)
        for b in range(rows // BLOCK):
            keys = slice(h * rows + b * BLOCK, (h + 1) * rows)
            out_ref[part(b), cols] = acc_ref[part(b), cols] * shrink_ref[part(b), cols] + jnp.dot(
                far_ref[part(b), keys], v2_ref[b * BLOCK : rows, cols], preferred_element_type=F32
            )
    groups, taps = filt_ref.shape
    tap = lax.broadcasted_iota(jnp.int32, (taps, 2 * taps), 0)
    ext = lax.broadcasted_iota(jnp.int32, (taps, 2 * taps), 1)
    flip = jnp.where(ext == taps - tap, 1.0, 0.0).astype(BF16)
    base = jnp.dot(filt_ref[...], flip, preferred_element_type=F32)
    for g in range(groups):
        row = jnp.broadcast_to(base[g : g + 1, :], (taps, 2 * taps))
        shifted = pltpu.roll(row, 0, 1, stride=1, stride_axis=0)
        table_ref[g * taps : (g + 1) * taps, :] = shifted.astype(BF16)
    for i in range(9):
        coef_ref[i : i + 1, :] = short_ref[i // 3, i % 3 : i % 3 + 1, :]
    coef_ref[9:10, :] = gain_ref[...]


def row_squares(att):
    af = att.astype(F32)
    af = af * af
    high = af.astype(BF16)
    low = (af - high.astype(F32)).astype(BF16)
    ones = jnp.ones((8, af.shape[1]), BF16)
    dims = (((1,), (1,)), ((), ()))
    return lax.dot_general(ones, high, dims, preferred_element_type=F32) + lax.dot_general(
        ones, low, dims, preferred_element_type=F32
    )


def values_kernel(
    near_ref, inv_ref, acc_ref, k2_ref, v2_ref, k1_ref, v1_ref, tails_ref, out_ref, halo_out, sq_ref
):
    rows, channels = out_ref.shape
    heads = channels // HEAD_DIM
    blocks = rows // BLOCK
    shift = BLOCK - HALO
    sq_ref[:, 0, :BLOCK] = jnp.zeros((sq_ref.shape[0], BLOCK), F32)
    hr = lax.broadcasted_iota(jnp.int32, (HALO, BLOCK), 0)
    hc = lax.broadcasted_iota(jnp.int32, (HALO, BLOCK), 1)
    tr = lax.broadcasted_iota(jnp.int32, (HALO, TAIL), 0)
    tc = lax.broadcasted_iota(jnp.int32, (HALO, TAIL), 1)
    units = []
    for h in range(heads):
        cols = cols_of(h)
        q = v1_ref[rows : rows + HALO, cols]
        k3 = jnp.where(is_even(), tails_ref[:TAIL, cols], k1_ref[rows:, cols])
        v3 = jnp.where(is_even(), tails_ref[TAIL:, cols], v1_ref[rows + HALO :, cols])
        near = [(k1_ref[part(j), cols], v1_ref[part(j), cols], None) for j in range(blocks)]
        near[-1] = (*near[-1][:2], hc <= hr + shift)
        middle = [(k2_ref[part(j), cols], v2_ref[part(j), cols], None) for j in range(blocks)]
        groups = [
            (near, absent(1)),
            (middle, absent(2)),
            ([(k3, v3, tc > tr + TAIL - HALO)], absent(3)),
        ]
        units.append((q, groups, None))

    def main(b):
        for h in range(heads):
            cols = cols_of(h)
            total = acc_ref[part(b), cols] + jnp.dot(
                near_ref[part(b), h * rows : (h + 1) * rows], v1_ref[:rows, cols],
                preferred_element_type=F32,
            )
            out_ref[part(b), cols] = (total * inv_ref[part(b), cols]).astype(BF16)
        sq_ref[:, 0, part(b + 1)] = row_squares(out_ref[part(b), :])

    ahead = [peak_of(unit) for unit in units]
    for i in range(max(heads, blocks)):
        if i < blocks:
            main(i)
        if i < heads:
            att = finish(weigh(units[i], *ahead[i]))
            halo_out[:, cols_of(i)] = jnp.where(
                lax.axis_index("ctx") >= 1, att, jnp.zeros(att.shape, BF16)
            )
    sq_ref[:, 0, :HALO] = row_squares(halo_out[...])


def mix_kernel(
    total_channels, sq_ref, halo_ref, att_ref, coef_ref, table_ref, out_ref, ext_ref, prod_ref, query_ref
):
    rows, channels = att_ref.shape
    taps = table_ref.shape[1] // 2
    per_lane_tile = 128 * table_ref.shape[0] // (taps * channels)
    summed = jnp.sum(sq_ref[:, 0, :], axis=0, keepdims=True)
    inverse = jnp.broadcast_to(lax.rsqrt(summed / total_channels + EPS), (8, summed.shape[1]))
    high = inverse.astype(BF16)
    rest = inverse - high.astype(F32)
    middle = rest.astype(BF16)
    low = (rest - middle.astype(F32)).astype(BF16)
    first = lax.broadcasted_iota(jnp.int32, (8, 128), 0) == 0
    ones = jnp.where(first, 1.0, 0.0).astype(BF16)
    dims = (((0,), (0,)), ((), ()))
    columns = (
        lax.dot_general(high, ones, dims, preferred_element_type=F32)
        + lax.dot_general(middle, ones, dims, preferred_element_type=F32)
    ) + lax.dot_general(low, ones, dims, preferred_element_type=F32)
    for ref, at, size, start in ((halo_ref, 0, HALO, 0), (att_ref, HALO, rows, BLOCK)):
        for w in range(0, channels, 128):
            lanes = slice(w, w + 128)
            normed = (
                ref[:, lanes].astype(F32) * columns[start : start + size] * coef_ref[9:10, lanes]
            ).astype(BF16)
            ext_ref[at : at + size, lanes] = normed.astype(F32)

    for w in range(0, channels, 128):
        lanes = slice(w, w + 128)
        for r in range(0, rows + taps, taps):
            start = HALO - taps + r
            shifted = [ext_ref[start - t : start - t + taps, lanes] for t in range(3)]
            branch = []
            for b in range(3):
                total = coef_ref[3 * b : 3 * b + 1, lanes] * shifted[0]
                for t in range(1, 3):
                    total = total + coef_ref[3 * b + t : 3 * b + t + 1, lanes] * shifted[t]
                branch.append(total)
            prod_ref[r : r + taps, lanes] = (branch[1] * branch[2]).astype(BF16)
            if r >= taps:
                query_ref[r - taps : r, lanes] = branch[0]
    group = lax.broadcasted_iota(jnp.int32, (taps, 128), 1) // (128 // per_lane_tile)
    n = taps * per_lane_tile
    for w in range(0, channels, 128):
        lanes = slice(w, w + 128)
        at = (w // 128) * n
        for r in range(0, rows, 2 * taps):
            pair = jnp.concatenate(
                [prod_ref[r + d : r + d + 2 * taps, lanes] for d in (0, taps)], axis=1
            )
            mixed = jnp.dot(table_ref[at : at + n, :], pair, preferred_element_type=F32)
            for i in range(2):
                ri = r + i * taps
                long_mix = mixed[:taps, i * 128 : (i + 1) * 128]
                for g in range(1, per_lane_tile):
                    long_mix = jnp.where(
                        group == g, mixed[g * taps : (g + 1) * taps, i * 128 : (i + 1) * 128], long_mix
                    )
                out_ref[ri : ri + taps, lanes] = (
                    att_ref[ri : ri + taps, lanes].astype(F32) + query_ref[ri : ri + taps, lanes] * long_mix
                ).astype(BF16)


def array(*dims, dtype=BF16):
    return jax.ShapeDtypeStruct(dims, dtype)


def call(kernel, out_shape, args, scratch=(), flops=0, mib=8, spec=VMEM):
    outs = out_shape if isinstance(out_shape, tuple) else (out_shape,)
    nbytes = sum(math.prod(a.shape) * a.dtype.itemsize for a in (*args, *outs))
    result = pl.pallas_call(
        kernel,
        out_shape=outs,
        in_specs=[spec] * len(args),
        out_specs=tuple(VMEM for _ in outs),
        scratch_shapes=list(scratch),
        cost_estimate=pl.CostEstimate(flops=flops, bytes_accessed=nbytes, transcendentals=0),
        compiler_params=pltpu.CompilerParams(vmem_limit_bytes=mib << 20),
    )(*args)
    return result if isinstance(out_shape, tuple) else result[0]


def per_device(queries, keys, values, norm_gain, short_filters, medium_filters):
    rows, channels = queries.shape
    taps, groups = medium_filters.shape
    count = lax.axis_size("ctx")
    peers = lax.axis_size("fsdp")
    heads = channels // HEAD_DIM
    ahead = [(i, i + 2) for i in range(count - 2)]
    beside = [(i, i ^ 1) for i in range(count)]

    behind_three = [(i, i + 3) for i in range(1, count - 3, 2)]

    half = array(rows, channels)
    full = array(rows, channels, dtype=F32)
    k2 = lax.ppermute(keys, "ctx", ahead)
    vq = jnp.concatenate([values, queries[rows - HALO :]], axis=0)
    vq2 = lax.ppermute(vq, "ctx", ahead)
    tails = jnp.concatenate([keys[rows - TAIL :], values[rows - TAIL :]], axis=0)
    tails3 = lax.ppermute(tails, "ctx", behind_three)
    pick = functools.partial(pick_kernel, rows)
    picked = call(pick, array(rows + TAIL, channels), (keys, k2))
    k1 = lax.ppermute(picked, "ctx", beside)
    peak, total, acc = call(
        early_kernel, (full, full, full), (queries, keys, vq), flops=300 << 20, mib=12
    )
    wide = array(rows, heads * rows)
    p_near, p_far, shrink, inverse = call(
        score_kernel, (wide, wide, full, full), (queries, k2, k1, peak, total),
        flops=400 << 20, mib=16,
    )
    picked = call(pick, array(rows + HALO + TAIL, channels), (vq, vq2))
    v1 = lax.ppermute(picked, "ctx", beside)
    acc, table, coef = call(
        far_values_kernel,
        (full, array(groups * taps, 2 * taps), array(16, channels, dtype=F32)),
        (
            p_far, shrink, acc, vq2,
            medium_filters.T, short_filters, norm_gain.reshape(1, channels),
        ),
        flops=200 << 20, mib=12,
    )
    attended, halo, squares = call(
        values_kernel, (half, array(HALO, channels), array(peers, 1, BLOCK + rows, dtype=F32)),
        (p_near, inverse, acc, k2, vq2, k1, v1, tails3), flops=500 << 20, mib=16,
    )
    shared = lax.all_to_all(squares, "fsdp", 0, 0, tiled=True)
    return call(
        functools.partial(mix_kernel, channels * peers), half,
        (shared, halo, attended, coef, table),
        scratch=(
            pltpu.VMEM((rows + HALO, channels), F32),
            pltpu.VMEM((rows + taps, channels), BF16),
            pltpu.VMEM((rows, channels), F32),
        ),
        flops=1 << 30, mib=12,
    )


def solution(mesh):
    placed = (
        P("ctx", "fsdp"),
        P("ctx", "fsdp"),
        P("ctx", "fsdp"),
        P("fsdp"),
        P(None, None, "fsdp"),
        P(None, "fsdp"),
    )

    return jax.shard_map(
        per_device, mesh=mesh, in_specs=placed, out_specs=P("ctx", "fsdp"), check_vma=False
    )
```

```python
import functools
import math

import jax
import jax.numpy as jnp
from jax import lax
from jax.experimental import pallas as pl
from jax.experimental.pallas import tpu as pltpu
from jax.sharding import PartitionSpec as P


HEAD_DIM = 128
BLOCK = 256
HALO = 144
TAIL = 128
NEG = -1e30
EPS = 1e-6
LOG2E = 1.4426950408889634
SCALE = LOG2E / math.sqrt(HEAD_DIM)
VMEM = pl.BlockSpec(memory_space=pltpu.VMEM)
HBM = pl.BlockSpec(memory_space=pltpu.HBM)
F32 = jnp.float32
BF16 = jnp.bfloat16


def cols_of(h):
    return slice(h * HEAD_DIM, (h + 1) * HEAD_DIM)


def peak_of(unit):
    q, groups, state = unit
    rows = q.shape[0]
    scores = []
    peak = None
    for pieces, gone in groups:
        top = None
        for k, v, mask in pieces:
            s = lax.dot_general(q, k, (((1,), (1,)), ((), ())), preferred_element_type=F32)
            if mask is not None:
                s = jnp.where(mask, s, NEG)
            scores.append((s, v, gone))
            for w in range(0, s.shape[1], 128):
                piece = s[:, w : w + 128]
                top = piece if top is None else jnp.maximum(top, piece)
        if gone is not None:
            top = top - gone
        peak = top if peak is None else jnp.maximum(peak, top)
    peak = jnp.broadcast_to(jnp.max(peak, axis=1, keepdims=True), (rows, 128))
    if state is not None:
        peak = jnp.maximum(state[0], peak)
    return scores, peak


def weigh(unit, scores, peak):
    total = acc = None
    if unit[2] is not None:
        before, total, acc = unit[2]
        shrink = jnp.exp2((before - peak) * SCALE)
        total, acc = total * shrink, acc * shrink
    for s, v, gone in scores:
        off = peak if gone is None else peak + gone
        halves = []
        for w in range(0, s.shape[1], 128):
            p = jnp.exp2((s[:, w : w + 128] - off) * SCALE)
            total = p if total is None else total + p
            halves.append(p.astype(BF16))
        o = jnp.dot(jnp.concatenate(halves, axis=1) if len(halves) > 1 else halves[0], v, preferred_element_type=F32)
        acc = o if acc is None else acc + o
    return peak, total, acc


def exponents(unit, scores, peak):
    shrink = total = None
    if unit[2] is not None:
        shrink = jnp.exp2((unit[2][0] - peak) * SCALE)
        total = unit[2][1] * shrink
    pieces = []
    for s, _, gone in scores:
        off = peak if gone is None else peak + gone
        for w in range(0, s.shape[1], 128):
            p = jnp.exp2((s[:, w : w + 128] - off) * SCALE)
            total = p if total is None else total + p
            pieces.append(p.astype(BF16))
    inverse = 1.0 / jnp.sum(total, axis=1, keepdims=True)
    return shrink, jnp.broadcast_to(inverse, total.shape), pieces


def run_units(units, then, done):
    ahead = peak_of(units[0][0])
    for i, (unit, tag) in enumerate(units):
        now = ahead
        if i + 1 < len(units):
            ahead = peak_of(units[i + 1][0])
        done(tag, then(unit, *now))


def finish(state):
    _, total, acc = state
    return (acc / jnp.sum(total, axis=1, keepdims=True)).astype(BF16)


def part(i):
    return slice(i * BLOCK, (i + 1) * BLOCK)


def grid_iota():
    shape = (BLOCK, BLOCK)
    return lax.broadcasted_iota(jnp.int32, shape, 0), lax.broadcasted_iota(jnp.int32, shape, 1)


def absent(distance):
    return jnp.where(lax.axis_index("ctx") >= distance, 0.0, -NEG).astype(F32)


def is_even():
    return lax.rem(lax.axis_index("ctx"), 2) == 0


def early_kernel(
    q_ref, k_ref, v_ref, peak_ref, total_ref, acc_ref,
):
    rows, channels = q_ref.shape
    ri, ci = grid_iota()
    units = []
    for h in range(channels // HEAD_DIM):
        cols = cols_of(h)
        for b in range(rows // BLOCK):
            pieces = [
                (k_ref[part(j), cols], v_ref[part(j), cols], ci <= ri if j == b else None)
                for j in range(b + 1)
            ]
            units.append(((q_ref[part(b), cols], [(pieces, None)], None), (part(b), cols)))

    def done(tag, state):
        peak_ref[tag], total_ref[tag], acc_ref[tag] = state

    run_units(units, weigh, done)


def pick_kernel(rows, own_ref, far_ref, *refs):
    out_ref = refs[-1]
    size = own_ref.shape[0]

    @pl.when(is_even())
    def _():
        out_ref[:size, :] = own_ref[...]
        out_ref[size:, :] = far_ref[rows - TAIL : rows, :]

    @pl.when(jnp.logical_not(is_even()))
    def _():
        out_ref[:size, :] = far_ref[...]


def score_kernel(
    q_ref, k2_ref, k1_ref, peak_in, total_in, near_ref, far_ref, shrink_ref, inv_ref
):
    rows, channels = q_ref.shape
    heads = channels // HEAD_DIM
    blocks = rows // BLOCK
    ri, ci = grid_iota()
    units = []
    for b in range(blocks):
        for h in range(heads):
            cols = cols_of(h)
            tag = (part(b), cols)
            near = [(k1_ref[part(j), cols], None, None) for j in range(blocks)]
            far = [
                (k2_ref[part(j), cols], None, ci > ri if j == b else None)
                for j in range(b, blocks)
            ]
            state = (peak_in[tag], total_in[tag], None)
            units.append(((q_ref[tag], [(near, absent(1)), (far, absent(2))], state), (b, h)))

    def done(tag, result):
        b, h = tag
        shrink, inverse, pieces = result
        shrink_ref[part(b), cols_of(h)] = shrink
        inv_ref[part(b), cols_of(h)] = inverse
        for i, p in enumerate(pieces):
            key = i * 128
            ref = near_ref
            if key >= rows:
                ref, key = far_ref, key - rows + b * BLOCK
            ref[part(b), h * rows + key : h * rows + key + 128] = p

    run_units(units, exponents, done)


def far_values_kernel(
    far_ref, shrink_ref, acc_ref, v2_ref, filt_ref, short_ref, gain_ref, out_ref, table_ref, coef_ref
):
    rows, channels = acc_ref.shape
    for h in range(channels // HEAD_DIM):
        cols = cols_of(h)
        for b in range(rows // BLOCK):
            keys = slice(h * rows + b * BLOCK, (h + 1) * rows)
            out_ref[part(b), cols] = acc_ref[part(b), cols] * shrink_ref[part(b), cols] + jnp.dot(
                far_ref[part(b), keys], v2_ref[b * BLOCK : rows, cols], preferred_element_type=F32
            )
    groups, taps = filt_ref.shape
    tap = lax.broadcasted_iota(jnp.int32, (taps, 2 * taps), 0)
    ext = lax.broadcasted_iota(jnp.int32, (taps, 2 * taps), 1)
    flip = jnp.where(ext == taps - tap, 1.0, 0.0).astype(BF16)
    base = jnp.dot(filt_ref[...], flip, preferred_element_type=F32)
    for g in range(groups):
        row = jnp.broadcast_to(base[g : g + 1, :], (taps, 2 * taps))
        shifted = pltpu.roll(row, 0, 1, stride=1, stride_axis=0)
        table_ref[g * taps : (g + 1) * taps, :] = shifted.astype(BF16)
    for i in range(9):
        coef_ref[i : i + 1, :] = short_ref[i // 3, i % 3 : i % 3 + 1, :]
    coef_ref[9:10, :] = gain_ref[...]


def row_squares(att):
    af = att.astype(F32)
    af = af * af
    high = af.astype(BF16)
    low = (af - high.astype(F32)).astype(BF16)
    ones = jnp.ones((8, af.shape[1]), BF16)
    dims = (((1,), (1,)), ((), ()))
    return lax.dot_general(ones, high, dims, preferred_element_type=F32) + lax.dot_general(
        ones, low, dims, preferred_element_type=F32
    )


def values_kernel(
    near_ref, inv_ref, acc_ref, k2_ref, v2_ref, k1_ref, v1_ref, tails_ref, out_ref, halo_out, sq_ref
):
    rows, channels = out_ref.shape
    heads = channels // HEAD_DIM
    blocks = rows // BLOCK
    shift = BLOCK - HALO
    sq_ref[:, 0, :BLOCK] = jnp.zeros((sq_ref.shape[0], BLOCK), F32)
    hr = lax.broadcasted_iota(jnp.int32, (HALO, BLOCK), 0)
    hc = lax.broadcasted_iota(jnp.int32, (HALO, BLOCK), 1)
    tr = lax.broadcasted_iota(jnp.int32, (HALO, TAIL), 0)
    tc = lax.broadcasted_iota(jnp.int32, (HALO, TAIL), 1)
    units = []
    for h in range(heads):
        cols = cols_of(h)
        q = v1_ref[rows : rows + HALO, cols]
        k3 = jnp.where(is_even(), tails_ref[:TAIL, cols], k1_ref[rows:, cols])
        v3 = jnp.where(is_even(), tails_ref[TAIL:, cols], v1_ref[rows + HALO :, cols])
        near = [(k1_ref[part(j), cols], v1_ref[part(j), cols], None) for j in range(blocks)]
        near[-1] = (*near[-1][:2], hc <= hr + shift)
        middle = [(k2_ref[part(j), cols], v2_ref[part(j), cols], None) for j in range(blocks)]
        groups = [
            (near, absent(1)),
            (middle, absent(2)),
            ([(k3, v3, tc > tr + TAIL - HALO)], absent(3)),
        ]
        units.append((q, groups, None))

    def main(b):
        for h in range(heads):
            cols = cols_of(h)
            total = acc_ref[part(b), cols] + jnp.dot(
                near_ref[part(b), h * rows : (h + 1) * rows], v1_ref[:rows, cols],
                preferred_element_type=F32,
            )
            out_ref[part(b), cols] = (total * inv_ref[part(b), cols]).astype(BF16)

    def halo_rows(h, ahead):
        att = finish(weigh(units[h], *ahead))
        halo_out[:, cols_of(h)] = jnp.where(
            lax.axis_index("ctx") >= 1, att, jnp.zeros(att.shape, BF16)
        )

    ahead = peak_of(units[0])
    for h in range(heads):
        now = ahead
        if h + 1 < heads:
            ahead = peak_of(units[h + 1])
        if h < blocks:
            main(h)
        halo_rows(h, now)
    for b in range(heads, blocks):
        main(b)
    for b in range(blocks):
        sq_ref[:, 0, part(b + 1)] = row_squares(out_ref[part(b), :])
    sq_ref[:, 0, :HALO] = row_squares(halo_out[...])


def mix_kernel(
    total_channels, sq_ref, halo_ref, att_ref, coef_ref, table_ref, out_ref, ext_ref, prod_ref, query_ref,
    mixed_ref, sems,
):
    rows, channels = att_ref.shape
    taps = table_ref.shape[1] // 2
    per_lane_tile = 128 * table_ref.shape[0] // (taps * channels)
    summed = jnp.sum(sq_ref[:, 0, :], axis=0, keepdims=True)
    inverse = jnp.broadcast_to(lax.rsqrt(summed / total_channels + EPS), (8, summed.shape[1]))
    high = inverse.astype(BF16)
    rest = inverse - high.astype(F32)
    middle = rest.astype(BF16)
    low = (rest - middle.astype(F32)).astype(BF16)
    first = lax.broadcasted_iota(jnp.int32, (8, 128), 0) == 0
    ones = jnp.where(first, 1.0, 0.0).astype(BF16)
    dims = (((0,), (0,)), ((), ()))
    columns = (
        lax.dot_general(high, ones, dims, preferred_element_type=F32)
        + lax.dot_general(middle, ones, dims, preferred_element_type=F32)
    ) + lax.dot_general(low, ones, dims, preferred_element_type=F32)
    for ref, at, size, start in ((halo_ref, 0, HALO, 0), (att_ref, HALO, rows, BLOCK)):
        for w in range(0, channels, 128):
            lanes = slice(w, w + 128)
            normed = (
                ref[:, lanes].astype(F32) * columns[start : start + size] * coef_ref[9:10, lanes]
            ).astype(BF16)
            ext_ref[at : at + size, lanes] = normed.astype(F32)

    for w in range(0, channels, 128):
        lanes = slice(w, w + 128)
        for r in range(0, rows + taps, taps):
            start = HALO - taps + r
            shifted = [ext_ref[start - t : start - t + taps, lanes] for t in range(3)]
            branch = []
            for b in range(3):
                total = coef_ref[3 * b : 3 * b + 1, lanes] * shifted[0]
                for t in range(1, 3):
                    total = total + coef_ref[3 * b + t : 3 * b + t + 1, lanes] * shifted[t]
                branch.append(total)
            prod_ref[r : r + taps, lanes] = (branch[1] * branch[2]).astype(BF16)
            if r >= taps:
                query_ref[r - taps : r, lanes] = branch[0]
    group = lax.broadcasted_iota(jnp.int32, (taps, 128), 1) // (128 // per_lane_tile)
    n = taps * per_lane_tile
    copies = []
    for r in range(0, rows, 2 * taps):
        for w in range(0, channels, 128):
            lanes = slice(w, w + 128)
            at = (w // 128) * n
            pair = jnp.concatenate(
                [prod_ref[r + d : r + d + 2 * taps, lanes] for d in (0, taps)], axis=1
            )
            mixed = jnp.dot(table_ref[at : at + n, :], pair, preferred_element_type=F32)
            for i in range(2):
                ri = r + i * taps
                long_mix = mixed[:taps, i * 128 : (i + 1) * 128]
                for g in range(1, per_lane_tile):
                    long_mix = jnp.where(
                        group == g, mixed[g * taps : (g + 1) * taps, i * 128 : (i + 1) * 128], long_mix
                    )
                mixed_ref[ri : ri + taps, lanes] = (
                    att_ref[ri : ri + taps, lanes].astype(F32)
                    + query_ref[ri : ri + taps, lanes] * long_mix
                ).astype(BF16)
        at = slice(r, r + 2 * taps)
        copies.append(
            pltpu.make_async_copy(mixed_ref.at[at, :], out_ref.at[at, :], sems.at[len(copies)])
        )
        copies[-1].start()
    for copy in copies:
        copy.wait()


def array(*dims, dtype=BF16):
    return jax.ShapeDtypeStruct(dims, dtype)


def call(kernel, out_shape, args, scratch=(), flops=0, mib=8, out_spec=VMEM):
    outs = out_shape if isinstance(out_shape, tuple) else (out_shape,)
    nbytes = sum(math.prod(a.shape) * a.dtype.itemsize for a in (*args, *outs))
    result = pl.pallas_call(
        kernel,
        out_shape=outs,
        in_specs=[VMEM] * len(args),
        out_specs=tuple(out_spec for _ in outs),
        scratch_shapes=list(scratch),
        cost_estimate=pl.CostEstimate(flops=flops, bytes_accessed=nbytes, transcendentals=0),
        compiler_params=pltpu.CompilerParams(vmem_limit_bytes=mib << 20),
    )(*args)
    return result if isinstance(out_shape, tuple) else result[0]


def per_device(queries, keys, values, norm_gain, short_filters, medium_filters):
    rows, channels = queries.shape
    taps, groups = medium_filters.shape
    count = lax.axis_size("ctx")
    peers = lax.axis_size("fsdp")
    heads = channels // HEAD_DIM
    ahead = [(i, i + 2) for i in range(count - 2)]
    beside = [(i, i ^ 1) for i in range(count)]

    behind_three = [(i, i + 3) for i in range(1, count - 3, 2)]

    half = array(rows, channels)
    full = array(rows, channels, dtype=F32)
    k2 = lax.ppermute(keys, "ctx", ahead)
    vq = jnp.concatenate([values, queries[rows - HALO :]], axis=0)
    vq2 = lax.ppermute(vq, "ctx", ahead)
    tails = jnp.concatenate([keys[rows - TAIL :], values[rows - TAIL :]], axis=0)
    tails3 = lax.ppermute(tails, "ctx", behind_three)
    pick = functools.partial(pick_kernel, rows)
    picked = call(pick, array(rows + TAIL, channels), (keys, k2))
    k1 = lax.ppermute(picked, "ctx", beside)
    peak, total, acc = call(
        early_kernel, (full, full, full), (queries, keys, vq), flops=300 << 20, mib=12
    )
    wide = array(rows, heads * rows)
    p_near, p_far, shrink, inverse = call(
        score_kernel, (wide, wide, full, full), (queries, k2, k1, peak, total),
        flops=400 << 20, mib=16,
    )
    picked = call(pick, array(rows + HALO + TAIL, channels), (vq, vq2))
    v1 = lax.ppermute(picked, "ctx", beside)
    acc, table, coef = call(
        far_values_kernel,
        (full, array(groups * taps, 2 * taps), array(16, channels, dtype=F32)),
        (
            p_far, shrink, acc, vq2,
            medium_filters.T, short_filters, norm_gain.reshape(1, channels),
        ),
        flops=200 << 20, mib=12,
    )
    attended, halo, squares = call(
        values_kernel, (half, array(HALO, channels), array(peers, 1, BLOCK + rows, dtype=F32)),
        (p_near, inverse, acc, k2, vq2, k1, v1, tails3), flops=500 << 20, mib=16,
    )
    shared = lax.all_to_all(squares, "fsdp", 0, 0, tiled=True)
    return call(
        functools.partial(mix_kernel, channels * peers), half,
        (shared, halo, attended, coef, table),
        scratch=(
            pltpu.VMEM((rows + HALO, channels), F32),
            pltpu.VMEM((rows + taps, channels), BF16),
            pltpu.VMEM((rows, channels), F32),
            pltpu.VMEM((rows, channels), BF16),
            pltpu.SemaphoreType.DMA((2,)),
        ),
        flops=1 << 30, mib=12, out_spec=pl.BlockSpec(memory_space=pl.ANY),
    )


def solution(mesh):
    placed = (
        P("ctx", "fsdp"),
        P("ctx", "fsdp"),
        P("ctx", "fsdp"),
        P("fsdp"),
        P(None, None, "fsdp"),
        P(None, "fsdp"),
    )

    return jax.shard_map(
        per_device, mesh=mesh, in_specs=placed, out_specs=P("ctx", "fsdp"), check_vma=False
    )
```

```python
import functools
import math

import jax
import jax.numpy as jnp
from jax import lax
from jax.experimental import pallas as pl
from jax.experimental.pallas import tpu as pltpu
from jax.sharding import PartitionSpec as P


HEAD_DIM = 128
BLOCK = 256
HALO = 144
TAIL = 128
NEG = -1e30
EPS = 1e-6
LOG2E = 1.4426950408889634
SCALE = LOG2E / math.sqrt(HEAD_DIM)
VMEM = pl.BlockSpec(memory_space=pltpu.VMEM)
HBM = pl.BlockSpec(memory_space=pltpu.HBM)
F32 = jnp.float32
BF16 = jnp.bfloat16


def cols_of(h):
    return slice(h * HEAD_DIM, (h + 1) * HEAD_DIM)


def peak_of(unit):
    q, groups, state = unit
    rows = q.shape[0]
    scores = []
    peak = None
    for pieces, gone in groups:
        top = None
        for k, v, mask in pieces:
            s = lax.dot_general(q, k, (((1,), (1,)), ((), ())), preferred_element_type=F32)
            if mask is not None:
                s = jnp.where(mask, s, NEG)
            scores.append((s, v, gone))
            for w in range(0, s.shape[1], 128):
                piece = s[:, w : w + 128]
                top = piece if top is None else jnp.maximum(top, piece)
        if gone is not None:
            top = top - gone
        peak = top if peak is None else jnp.maximum(peak, top)
    peak = jnp.broadcast_to(jnp.max(peak, axis=1, keepdims=True), (rows, 128))
    if state is not None:
        peak = jnp.maximum(state[0], peak)
    return scores, peak


def weigh(unit, scores, peak):
    total = acc = None
    if unit[2] is not None:
        before, total, acc = unit[2]
        shrink = jnp.exp2((before - peak) * SCALE)
        total, acc = total * shrink, acc * shrink
    for s, v, gone in scores:
        off = peak if gone is None else peak + gone
        halves = []
        for w in range(0, s.shape[1], 128):
            p = jnp.exp2((s[:, w : w + 128] - off) * SCALE)
            total = p if total is None else total + p
            halves.append(p.astype(BF16))
        o = jnp.dot(jnp.concatenate(halves, axis=1) if len(halves) > 1 else halves[0], v, preferred_element_type=F32)
        acc = o if acc is None else acc + o
    return peak, total, acc


def exponents(unit, scores, peak):
    shrink = total = None
    if unit[2] is not None:
        shrink = jnp.exp2((unit[2][0] - peak) * SCALE)
        total = unit[2][1] * shrink
    pieces = []
    for s, _, gone in scores:
        off = peak if gone is None else peak + gone
        for w in range(0, s.shape[1], 128):
            p = jnp.exp2((s[:, w : w + 128] - off) * SCALE)
            total = p if total is None else total + p
            pieces.append(p.astype(BF16))
    inverse = 1.0 / jnp.sum(total, axis=1, keepdims=True)
    return shrink, jnp.broadcast_to(inverse, total.shape), pieces


def run_units(units, then, done):
    ahead = peak_of(units[0][0])
    for i, (unit, tag) in enumerate(units):
        now = ahead
        if i + 1 < len(units):
            ahead = peak_of(units[i + 1][0])
        done(tag, then(unit, *now))


def finish(state):
    _, total, acc = state
    return (acc / jnp.sum(total, axis=1, keepdims=True)).astype(BF16)


def part(i):
    return slice(i * BLOCK, (i + 1) * BLOCK)


def grid_iota():
    shape = (BLOCK, BLOCK)
    return lax.broadcasted_iota(jnp.int32, shape, 0), lax.broadcasted_iota(jnp.int32, shape, 1)


def absent(distance):
    return jnp.where(lax.axis_index("ctx") >= distance, 0.0, -NEG).astype(F32)


def is_even():
    return lax.rem(lax.axis_index("ctx"), 2) == 0


def early_kernel(
    q_ref, k_ref, v_ref, peak_ref, total_ref, acc_ref,
):
    rows, channels = q_ref.shape
    ri, ci = grid_iota()
    units = []
    for h in range(channels // HEAD_DIM):
        cols = cols_of(h)
        for b in range(rows // BLOCK):
            pieces = [
                (k_ref[part(j), cols], v_ref[part(j), cols], ci <= ri if j == b else None)
                for j in range(b + 1)
            ]
            units.append(((q_ref[part(b), cols], [(pieces, None)], None), (part(b), cols)))

    def done(tag, state):
        peak_ref[tag], total_ref[tag], acc_ref[tag] = state

    run_units(units, weigh, done)


def pick_kernel(rows, own_ref, far_ref, *refs):
    out_ref = refs[-1]
    size = own_ref.shape[0]

    @pl.when(is_even())
    def _():
        out_ref[:size, :] = own_ref[...]
        out_ref[size:, :] = far_ref[rows - TAIL : rows, :]

    @pl.when(jnp.logical_not(is_even()))
    def _():
        out_ref[:size, :] = far_ref[...]


def score_kernel(
    q_ref, k2_ref, k1_ref, peak_in, total_in, near_ref, far_ref, shrink_ref, inv_ref
):
    rows, channels = q_ref.shape
    heads = channels // HEAD_DIM
    blocks = rows // BLOCK
    ri, ci = grid_iota()
    units = []
    for b in range(blocks):
        for h in range(heads):
            cols = cols_of(h)
            tag = (part(b), cols)
            near = [(k1_ref[part(j), cols], None, None) for j in range(blocks)]
            far = [
                (k2_ref[part(j), cols], None, ci > ri if j == b else None)
                for j in range(b, blocks)
            ]
            state = (peak_in[tag], total_in[tag], None)
            units.append(((q_ref[tag], [(near, absent(1)), (far, absent(2))], state), (b, h)))

    def done(tag, result):
        b, h = tag
        shrink, inverse, pieces = result
        shrink_ref[part(b), cols_of(h)] = shrink
        inv_ref[part(b), cols_of(h)] = inverse
        for i, p in enumerate(pieces):
            key = i * 128
            ref = near_ref
            if key >= rows:
                ref, key = far_ref, key - rows + b * BLOCK
            ref[part(b), h * rows + key : h * rows + key + 128] = p

    run_units(units, exponents, done)


def far_values_kernel(
    far_ref, shrink_ref, acc_ref, v2_ref, filt_ref, short_ref, gain_ref, out_ref, table_ref, coef_ref
):
    rows, channels = acc_ref.shape
    for h in range(channels // HEAD_DIM):
        cols = cols_of(h)
        for b in range(rows // BLOCK):
            keys = slice(h * rows + b * BLOCK, (h + 1) * rows)
            out_ref[part(b), cols] = acc_ref[part(b), cols] * shrink_ref[part(b), cols] + jnp.dot(
                far_ref[part(b), keys], v2_ref[b * BLOCK : rows, cols], preferred_element_type=F32
            )
    groups, taps = filt_ref.shape
    tap = lax.broadcasted_iota(jnp.int32, (taps, 2 * taps), 0)
    ext = lax.broadcasted_iota(jnp.int32, (taps, 2 * taps), 1)
    flip = jnp.where(ext == taps - tap, 1.0, 0.0).astype(BF16)
    base = jnp.dot(filt_ref[...], flip, preferred_element_type=F32)
    for g in range(groups):
        row = jnp.broadcast_to(base[g : g + 1, :], (taps, 2 * taps))
        shifted = pltpu.roll(row, 0, 1, stride=1, stride_axis=0)
        table_ref[g * taps : (g + 1) * taps, :] = shifted.astype(BF16)
    for i in range(9):
        coef_ref[i : i + 1, :] = short_ref[i // 3, i % 3 : i % 3 + 1, :]
    coef_ref[9:10, :] = gain_ref[...]


def row_squares(att):
    af = att.astype(F32)
    af = af * af
    high = af.astype(BF16)
    low = (af - high.astype(F32)).astype(BF16)
    ones = jnp.ones((8, af.shape[1]), BF16)
    dims = (((1,), (1,)), ((), ()))
    return lax.dot_general(ones, high, dims, preferred_element_type=F32) + lax.dot_general(
        ones, low, dims, preferred_element_type=F32
    )


def values_kernel(
    near_ref, inv_ref, acc_ref, k2_ref, v2_ref, k1_ref, v1_ref, tails_ref, out_ref, halo_out, sq_ref
):
    rows, channels = out_ref.shape
    heads = channels // HEAD_DIM
    blocks = rows // BLOCK
    shift = BLOCK - HALO
    sq_ref[:, 0, :BLOCK] = jnp.zeros((sq_ref.shape[0], BLOCK), F32)
    hr = lax.broadcasted_iota(jnp.int32, (HALO, BLOCK), 0)
    hc = lax.broadcasted_iota(jnp.int32, (HALO, BLOCK), 1)
    tr = lax.broadcasted_iota(jnp.int32, (HALO, TAIL), 0)
    tc = lax.broadcasted_iota(jnp.int32, (HALO, TAIL), 1)
    units = []
    for h in range(heads):
        cols = cols_of(h)
        q = v1_ref[rows : rows + HALO, cols]
        k3 = jnp.where(is_even(), tails_ref[:TAIL, cols], k1_ref[rows:, cols])
        v3 = jnp.where(is_even(), tails_ref[TAIL:, cols], v1_ref[rows + HALO :, cols])
        near = [(k1_ref[part(j), cols], v1_ref[part(j), cols], None) for j in range(blocks)]
        near[-1] = (*near[-1][:2], hc <= hr + shift)
        middle = [(k2_ref[part(j), cols], v2_ref[part(j), cols], None) for j in range(blocks)]
        groups = [
            (near, absent(1)),
            (middle, absent(2)),
            ([(k3, v3, tc > tr + TAIL - HALO)], absent(3)),
        ]
        units.append((q, groups, None))

    def main(b):
        for h in range(heads):
            cols = cols_of(h)
            total = acc_ref[part(b), cols] + jnp.dot(
                near_ref[part(b), h * rows : (h + 1) * rows], v1_ref[:rows, cols],
                preferred_element_type=F32,
            )
            out_ref[part(b), cols] = (total * inv_ref[part(b), cols]).astype(BF16)

    def halo_rows(h, ahead):
        att = finish(weigh(units[h], *ahead))
        halo_out[:, cols_of(h)] = jnp.where(
            lax.axis_index("ctx") >= 1, att, jnp.zeros(att.shape, BF16)
        )

    ahead = peak_of(units[0])
    for h in range(heads):
        now = ahead
        if h + 1 < heads:
            ahead = peak_of(units[h + 1])
        if h < blocks:
            main(h)
        halo_rows(h, now)
    for b in range(heads, blocks):
        main(b)
    for b in range(blocks):
        sq_ref[:, 0, part(b + 1)] = row_squares(out_ref[part(b), :])
    sq_ref[:, 0, :HALO] = row_squares(halo_out[...])


def mix_kernel(
    total_channels, sq_ref, halo_ref, att_ref, coef_ref, table_ref, out_ref, ext_ref, prod_ref, query_ref,
    mixed_ref, sems,
):
    rows, channels = att_ref.shape
    taps = table_ref.shape[1] // 2
    per_lane_tile = 128 * table_ref.shape[0] // (taps * channels)
    summed = jnp.sum(sq_ref[:, 0, :], axis=0, keepdims=True)
    inverse = jnp.broadcast_to(lax.rsqrt(summed / total_channels + EPS), (8, summed.shape[1]))
    high = inverse.astype(BF16)
    rest = inverse - high.astype(F32)
    middle = rest.astype(BF16)
    low = (rest - middle.astype(F32)).astype(BF16)
    row = lax.broadcasted_iota(jnp.int32, inverse.shape, 0)
    terms = jnp.where(
        row == 0, high.astype(F32), jnp.where(row == 1, middle.astype(F32), low.astype(F32))
    ).astype(BF16)
    ones = jnp.where(lax.broadcasted_iota(jnp.int32, (8, 128), 0) < 3, 1.0, 0.0).astype(BF16)
    columns = lax.dot_general(
        terms, ones, (((0,), (0,)), ((), ())), preferred_element_type=F32
    )
    for ref, at, size, start in ((halo_ref, 0, HALO, 0), (att_ref, HALO, rows, BLOCK)):
        for w in range(0, channels, 128):
            lanes = slice(w, w + 128)
            normed = (
                ref[:, lanes].astype(F32) * columns[start : start + size] * coef_ref[9:10, lanes]
            ).astype(BF16)
            ext_ref[at : at + size, lanes] = normed.astype(F32)

    for w in range(0, channels, 128):
        lanes = slice(w, w + 128)
        for r in range(0, rows + taps, taps):
            start = HALO - taps + r
            shifted = [ext_ref[start - t : start - t + taps, lanes] for t in range(3)]
            branch = []
            for b in range(3):
                total = coef_ref[3 * b : 3 * b + 1, lanes] * shifted[0]
                for t in range(1, 3):
                    total = total + coef_ref[3 * b + t : 3 * b + t + 1, lanes] * shifted[t]
                branch.append(total)
            prod_ref[r : r + taps, lanes] = (branch[1] * branch[2]).astype(BF16)
            if r >= taps:
                query_ref[r - taps : r, lanes] = branch[0]
    group = lax.broadcasted_iota(jnp.int32, (taps, 128), 1) // (128 // per_lane_tile)
    n = taps * per_lane_tile
    copies = []
    for r in range(0, rows, 2 * taps):
        for w in range(0, channels, 128):
            lanes = slice(w, w + 128)
            at = (w // 128) * n
            pair = jnp.concatenate(
                [prod_ref[r + d : r + d + 2 * taps, lanes] for d in (0, taps)], axis=1
            )
            mixed = jnp.dot(table_ref[at : at + n, :], pair, preferred_element_type=F32)
            for i in range(2):
                ri = r + i * taps
                long_mix = mixed[:taps, i * 128 : (i + 1) * 128]
                for g in range(1, per_lane_tile):
                    long_mix = jnp.where(
                        group == g, mixed[g * taps : (g + 1) * taps, i * 128 : (i + 1) * 128], long_mix
                    )
                mixed_ref[ri : ri + taps, lanes] = (
                    att_ref[ri : ri + taps, lanes].astype(F32)
                    + query_ref[ri : ri + taps, lanes] * long_mix
                ).astype(BF16)
        at = slice(r, r + 2 * taps)
        copies.append(
            pltpu.make_async_copy(mixed_ref.at[at, :], out_ref.at[at, :], sems.at[len(copies)])
        )
        copies[-1].start()
    for copy in copies:
        copy.wait()


def array(*dims, dtype=BF16):
    return jax.ShapeDtypeStruct(dims, dtype)


def call(kernel, out_shape, args, scratch=(), flops=0, mib=8, out_spec=VMEM):
    outs = out_shape if isinstance(out_shape, tuple) else (out_shape,)
    nbytes = sum(math.prod(a.shape) * a.dtype.itemsize for a in (*args, *outs))
    result = pl.pallas_call(
        kernel,
        out_shape=outs,
        in_specs=[VMEM] * len(args),
        out_specs=tuple(out_spec for _ in outs),
        scratch_shapes=list(scratch),
        cost_estimate=pl.CostEstimate(flops=flops, bytes_accessed=nbytes, transcendentals=0),
        compiler_params=pltpu.CompilerParams(vmem_limit_bytes=mib << 20),
    )(*args)
    return result if isinstance(out_shape, tuple) else result[0]


def per_device(queries, keys, values, norm_gain, short_filters, medium_filters):
    rows, channels = queries.shape
    taps, groups = medium_filters.shape
    count = lax.axis_size("ctx")
    peers = lax.axis_size("fsdp")
    heads = channels // HEAD_DIM
    ahead = [(i, i + 2) for i in range(count - 2)]
    beside = [(i, i ^ 1) for i in range(count)]

    behind_three = [(i, i + 3) for i in range(1, count - 3, 2)]

    half = array(rows, channels)
    full = array(rows, channels, dtype=F32)
    k2 = lax.ppermute(keys, "ctx", ahead)
    vq = jnp.concatenate([values, queries[rows - HALO :]], axis=0)
    vq2 = lax.ppermute(vq, "ctx", ahead)
    tails = jnp.concatenate([keys[rows - TAIL :], values[rows - TAIL :]], axis=0)
    tails3 = lax.ppermute(tails, "ctx", behind_three)
    pick = functools.partial(pick_kernel, rows)
    picked = call(pick, array(rows + TAIL, channels), (keys, k2))
    k1 = lax.ppermute(picked, "ctx", beside)
    peak, total, acc = call(
        early_kernel, (full, full, full), (queries, keys, vq), flops=300 << 20, mib=12
    )
    wide = array(rows, heads * rows)
    p_near, p_far, shrink, inverse = call(
        score_kernel, (wide, wide, full, full), (queries, k2, k1, peak, total),
        flops=400 << 20, mib=16,
    )
    picked = call(pick, array(rows + HALO + TAIL, channels), (vq, vq2))
    v1 = lax.ppermute(picked, "ctx", beside)
    acc, table, coef = call(
        far_values_kernel,
        (full, array(groups * taps, 2 * taps), array(16, channels, dtype=F32)),
        (
            p_far, shrink, acc, vq2,
            medium_filters.T, short_filters, norm_gain.reshape(1, channels),
        ),
        flops=200 << 20, mib=12,
    )
    attended, halo, squares = call(
        values_kernel, (half, array(HALO, channels), array(peers, 1, BLOCK + rows, dtype=F32)),
        (p_near, inverse, acc, k2, vq2, k1, v1, tails3), flops=500 << 20, mib=16,
    )
    shared = lax.all_to_all(squares, "fsdp", 0, 0, tiled=True)
    return call(
        functools.partial(mix_kernel, channels * peers), half,
        (shared, halo, attended, coef, table),
        scratch=(
            pltpu.VMEM((rows + HALO, channels), F32),
            pltpu.VMEM((rows + taps, channels), BF16),
            pltpu.VMEM((rows, channels), F32),
            pltpu.VMEM((rows, channels), BF16),
            pltpu.SemaphoreType.DMA((2,)),
        ),
        flops=1 << 30, mib=12, out_spec=pl.BlockSpec(memory_space=pl.ANY),
    )


def solution(mesh):
    placed = (
        P("ctx", "fsdp"),
        P("ctx", "fsdp"),
        P("ctx", "fsdp"),
        P("fsdp"),
        P(None, None, "fsdp"),
        P(None, "fsdp"),
    )

    return jax.shard_map(
        per_device, mesh=mesh, in_specs=placed, out_specs=P("ctx", "fsdp"), check_vma=False
    )
```
